32 devices in a mesh: mem: 8 (over y, x, core), tile: 4 (over z).
Axes of the slice: x: 2, y: 2, z: 4, core: 2. Of those that a mesh axis runs over, the one named last changes fastest.
Arguments:
- perturb: bfloat16 [16, 6, 16, 64, 128], P('mem', None, None, 'tile'), may hold values from -2.5 to 2.5
- alpha: float32 [16, 16, 64, 128], P('mem', None, 'tile'), may hold values from -5 to 5
- alpha_mom: float32 [16, 16, 64, 128], P('mem', None, 'tile'), may hold values from -6 to 6
- static_ctl: float32 [6, 16, 64, 128], P(None, None, 'tile'), may hold values from -6 to 6
- static_mom: float32 [6, 16, 64, 128], P(None, 'mem', 'tile'), may hold values from -6 to 6
- loc_coef: float32 [2, 64, 128], P(None, 'tile'), may hold values from 0.04 to 0.36, as said below
- static_coef: float32 [2, 64, 128], P(None, 'tile'), may hold values from 0.04 to 0.36, as said below
- obs_cell: int32 [4, 1024], P('tile'), may hold values from 0 to 2047
- obs_mask: int32 [4, 1024], P('tile'), may hold values 0 or 1
- obs_value: float32 [6, 16, 4, 1024], P(None, None, 'tile'), may hold values from -6 to 6
- obs_weight: float32 [6, 16, 4, 1024], P(None, None, 'tile'), may hold values from 0.3 to 3
Outputs:
- new_alpha: float32 [16, 16, 64, 128], P('mem', None, 'tile')
- new_alpha_mom: float32 [16, 16, 64, 128], P('mem', None, 'tile')
- new_static: float32 [6, 16, 64, 128], P(None, 'mem', 'tile')
- new_static_mom: float32 [6, 16, 64, 128], P(None, 'mem', 'tile')
The draws below stay inside these ranges and needn't reach their ends.
Inputs may be any that keep to these rules, and one draw needn't show every extreme that they name: `obs_cell`: slots of a tile may name the same cell. `loc_coef`: index 0 lies in 0.18 to 0.36, index 1 in 0.04 to 0.08. `static_coef`: index 0 lies in 0.18 to 0.36, index 1 in 0.04 to 0.08.
All inputs are finite; a program needn't handle non-finite values. No bound on the sum of `obs_mask` on one device may be relied on, other than what follows from the above.
Results may differ from the reference program's by a relative error of at most 0.0003.
Values sent between devices are 32-bit elements; how exact they have to be, the bound alone decides.
A program may use at most 64 MiB of HBM per device.

```python
import math
import jax
import jax.numpy as jnp
from jax import lax

VARIABLES = 6
LEVELS = 16
TILE_ROWS = 16
COLUMNS = 128
STATIONS = 1024
DIFF_STEPS = 12
MEMBERS = 16
TILE_COUNT = 4
GRID_ROWS = 64


log_two = 0.6931471805599453


def coefficient_field(key):
    uniform_part = jax.random.uniform(key, (2, GRID_ROWS, COLUMNS), jnp.float32)
    lowest = jnp.array([0.18, 0.04], jnp.float32)[:, None, None]
    return lowest * jnp.exp(uniform_part * log_two)


def draw_loc_coef(key, part):
    return coefficient_field(jax.random.fold_in(key, 11))


def draw_static_coef(key, part):
    return coefficient_field(jax.random.fold_in(key, 23))


def draw_alpha(key, part):
    layout = (MEMBERS, LEVELS, GRID_ROWS, COLUMNS)
    subkey = jax.random.fold_in(key, 37)
    return jnp.clip(0.8 + jax.random.normal(subkey, layout, jnp.float32), -5.0, 5.0)


def touch_ends(values, rng, low, high):
    place = [jax.random.randint(jax.random.fold_in(rng, axis), (), 0, length) for axis, length in enumerate(values.shape)]
    widest = values.shape.index(max(values.shape))
    beside = place[:widest] + [(place[widest] + 1) % values.shape[widest]] + place[widest + 1:]
    return values.at[tuple(place)].set(low).at[tuple(beside)].set(high)


def block_levels(own_key, dims, shards, least, top_value):
    def one(dim, parts):
        heights = jax.random.uniform(jax.random.fold_in(jax.random.fold_in(own_key, 6), dim), (parts,), jnp.float32, least / len(shards), top_value / len(shards))
        return jnp.repeat(jnp.exp(heights), dims[dim] // parts).reshape((-1,) + (1,) * (len(dims) - dim - 1))

    loudness = one(*shards[0])
    for cut in shards[1:]:
        loudness = loudness * one(*cut)
    return loudness


def normal_values(rng, extent, deviation, limit, split=(), kind=jnp.bfloat16):
    result = jax.random.normal(rng, extent, jnp.float32) * deviation
    if len(split) > 0:
        result = block_levels(rng, extent, split, -0.22, 0.18) * result
    return jnp.clip(result, min=-limit, max=limit).astype(kind)


def setup_inputs(seed: int = 0) -> dict:
    seeds = jax.random.split(jax.random.key(seed), 12)
    return {
        "perturb": normal_values(seeds[0], (MEMBERS, VARIABLES, LEVELS, GRID_ROWS, COLUMNS), 0.18, 2.5, ((0, 8), (3, 4))),
        "alpha": draw_alpha(jax.random.fold_in(seeds[11], 71), 0),
        "alpha_mom": normal_values(seeds[2], (MEMBERS, LEVELS, GRID_ROWS, COLUMNS), 0.5, 6.0, ((0, 8), (2, 4)), jnp.float32),
        "static_ctl": normal_values(seeds[3], (VARIABLES, LEVELS, GRID_ROWS, COLUMNS), 1.0, 6.0, ((2, 4),), jnp.float32),
        "static_mom": normal_values(seeds[4], (VARIABLES, LEVELS, GRID_ROWS, COLUMNS), 0.5, 6.0, ((1, 8), (2, 4)), jnp.float32),
        "loc_coef": draw_loc_coef(jax.random.fold_in(seeds[11], 71), 0),
        "static_coef": draw_static_coef(jax.random.fold_in(seeds[11], 71), 0),
        "obs_cell": touch_ends(jax.random.randint(seeds[7], (TILE_COUNT, STATIONS), 0, TILE_ROWS * COLUMNS), jax.random.fold_in(seeds[7], 1), 0, (TILE_ROWS * COLUMNS) - 1).astype(jnp.int32),
        "obs_mask": touch_ends((jax.random.randint(seeds[8], (TILE_COUNT, STATIONS), 0, 4) < 3).astype(jnp.int32), jax.random.fold_in(seeds[8], 1), 0, 1),
        "obs_value": normal_values(seeds[9], (VARIABLES, LEVELS, TILE_COUNT, STATIONS), 1.0, 6.0, ((2, 4),), jnp.float32),
        "obs_weight": jnp.clip(jnp.exp(math.log(3.0) - 2.3025851 * jax.random.uniform(seeds[10], (VARIABLES, LEVELS, TILE_COUNT, STATIONS), jnp.float32) ** block_levels(seeds[10], (VARIABLES, LEVELS, TILE_COUNT, STATIONS), ((2, 4),), -0.2, 0.2)), 0.3, 3.0),
    }


momentum_rate = 0.9
step_rate = 0.5

def smooth(padded, factors):
    faces_x = factors[0]
    faces_y = factors[1]
    flux_x = faces_x[:-1] * (padded[..., 1:, :] - padded[..., :-1, :])
    middle = padded[..., 1:-1, :]
    shifted = jnp.concatenate([middle[..., 1:], jnp.zeros_like(middle[..., :1])], axis=-1)
    flux_y = faces_y[1:-1] * (shifted - middle)
    flux_left = jnp.concatenate([jnp.zeros_like(flux_y[..., :1]), flux_y[..., :-1]], axis=-1)
    return middle + (flux_x[..., 1:, :] - flux_x[..., :-1, :]) + (flux_y - flux_left)

def diffuse(quantity, factors):
    padded_factors = jnp.pad(factors, ((0, 0), (1, 1), (0, 0)))
    widths = [(0, 0)] * (quantity.ndim - 2) + [(1, 1), (0, 0)]

    def advance(turn, current):
        return smooth(jnp.pad(current, widths), padded_factors)
    return lax.fori_loop(0, DIFF_STEPS, advance, quantity)

def reference(perturb, alpha, alpha_mom, static_ctl, static_mom, loc_coef, static_coef, obs_cell, obs_mask, obs_value, obs_weight):

    def add_member(running, pair):
        weights, member = pair
        localized = diffuse(weights, loc_coef)
        return (running + localized[None] * member.astype(jnp.float32), jnp.float32(0.0))
    ensemble, _ = lax.scan(add_member, jnp.zeros(static_ctl.shape, jnp.float32), (alpha, perturb))
    increment = ensemble + diffuse(static_ctl, static_coef)
    tile_total = obs_cell.shape[0]
    flat_index = (jnp.arange(tile_total, dtype=jnp.int32)[:, None] * (TILE_ROWS * COLUMNS) + obs_cell).reshape(-1).astype(jnp.int32)
    flattened = increment.reshape(VARIABLES, LEVELS, GRID_ROWS * COLUMNS)
    picked = jnp.take(flattened, flat_index, axis=2).reshape(VARIABLES, LEVELS, tile_total, STATIONS)
    misfit = obs_mask.astype(jnp.float32)[None, None] * obs_weight * (picked - obs_value)
    gradient = jnp.zeros_like(flattened).at[:, :, flat_index].add(misfit.reshape(VARIABLES, LEVELS, -1)).reshape(increment.shape)
    static_grad = static_ctl + diffuse(gradient, static_coef)

    def member_grad(carry, pair):
        weights, member = pair
        projected = lax.optimization_barrier(jnp.sum(member.astype(jnp.float32) * gradient, axis=0))
        return (carry, weights + diffuse(projected, loc_coef))
    _, alpha_grad = lax.scan(member_grad, jnp.float32(0.0), (alpha, perturb))
    new_alpha_mom = momentum_rate * alpha_mom + alpha_grad
    new_alpha = alpha - step_rate * new_alpha_mom
    new_static_mom = momentum_rate * static_mom + static_grad
    new_static = static_ctl - step_rate * new_static_mom
    return (new_alpha, new_alpha_mom, new_static, new_static_mom)
```

```python
import functools

import jax
import jax.numpy as jnp
from jax import lax
from jax.experimental import pallas as pl
from jax.experimental.pallas import tpu as pltpu
from jax.sharding import PartitionSpec as P

DIFF_STEPS = 12
LANES = 128
SUB = 8

momentum_rate = 0.9
step_rate = 0.5


def diffuse(src, bufs, coefs, height, block):
    center, down, right, left = coefs
    current = src
    for turn in range(DIFF_STEPS):
        target = bufs[turn % 2]
        low = turn + 1
        count = height + 2 * (DIFF_STEPS - 1 - turn)

        def rows(b, carry, current=current, target=target, low=low):
            i = low + b * block
            f = current[pl.ds(i, block)]
            above = current[pl.ds(i - 1, block)]
            below = current[pl.ds(i + 1, block)]
            new = center[pl.ds(i, block)] * f
            new = new + (down[pl.ds(i, block)] * below + down[pl.ds(i - 1, block)] * above)
            new = new + (
                right[pl.ds(i, block)] * pltpu.roll(f, LANES - 1, 3)
                + left[pl.ds(i, block)] * pltpu.roll(f, 1, 3)
            )
            target[pl.ds(i, block)] = new
            return carry

        lax.fori_loop(0, -(-count // block), rows, 0, unroll=True)
        current = target
    return current


def kernel(
    dims,
    perturb,
    alpha,
    loc_coef,
    static_coef,
    obs_cell,
    obs_mask,
    static_hbm,
    value_hbm,
    weight_hbm,
    out_alpha,
    out_static,
    field_a,
    field_b,
    ping_a0,
    ping_a1,
    field_s,
    field_g,
    ping_s0,
    ping_s1,
    coef_flat,
    coef_rows,
    coef_loc,
    coef_static,
    own_ctl,
    own_value,
    own_weight,
    matrix,
    obs_scale,
    obs_shift,
    static_flat,
    local_flat,
    part_own,
    part_pair,
    pair_in,
    chip_in,
    grads,
    load_sem,
    halo_send,
    halo_recv,
    pair_send,
    pair_recv,
    chip_send,
    chip_recv,
    gather_send,
    gather_recv,
    relay_send,
    relay_recv,
):
    mem_count, tile_count, members, variables, levels, height, stations = dims
    chips = mem_count // 2
    share = levels // mem_count
    fields = variables * share
    span = share * height
    static_vregs = field_s.shape[1]
    alpha_vregs = field_a.shape[1]
    mem = lax.axis_index("mem")
    tile = lax.axis_index("tile")
    chip = mem // 2
    core = lax.rem(mem, 2)
    partner = chip * 2 + (1 - core)
    first = mem * share
    halo = DIFF_STEPS
    has_low = tile > 0
    has_high = tile < tile_count - 1

    loads = [
        pltpu.make_async_copy(static_hbm.at[:, pl.ds(first, share)], own_ctl, load_sem.at[0]),
        pltpu.make_async_copy(value_hbm.at[:, pl.ds(first, share)], own_value, load_sem.at[1]),
        pltpu.make_async_copy(weight_hbm.at[:, pl.ds(first, share)], own_weight, load_sem.at[2]),
    ]
    for load in loads:
        load.start()

    barrier = pltpu.get_barrier_semaphore()
    pl.semaphore_signal(barrier, inc=1, device_id={"mem": partner})
    for k in range(1, chips):
        pl.semaphore_signal(
            barrier, inc=1, device_id={"mem": lax.rem(chip + k, chips) * 2 + core}
        )

    @pl.when(has_low)
    def _():
        pl.semaphore_signal(barrier, inc=1, device_id={"tile": tile - 1})

    @pl.when(has_high)
    def _():
        pl.semaphore_signal(barrier, inc=1, device_id={"tile": tile + 1})

    def up_copy(buf, slot):
        return pltpu.make_async_remote_copy(
            src_ref=buf.at[pl.ds(height, halo)],
            dst_ref=buf.at[pl.ds(0, halo)],
            send_sem=halo_send.at[slot, 0],
            recv_sem=halo_recv.at[slot, 0],
            device_id={"tile": tile + 1},
        )

    def down_copy(buf, slot):
        return pltpu.make_async_remote_copy(
            src_ref=buf.at[pl.ds(halo, halo)],
            dst_ref=buf.at[pl.ds(halo + height, halo)],
            send_sem=halo_send.at[slot, 1],
            recv_sem=halo_recv.at[slot, 1],
            device_id={"tile": tile - 1},
        )

    def halo_start(buf, slot):
        @pl.when(has_high)
        def _():
            up_copy(buf, slot).start()

        @pl.when(has_low)
        def _():
            down_copy(buf, slot).start()

    def halo_wait(buf, slot):
        @pl.when(has_high)
        def _():
            up_copy(buf, slot).wait_send()
            down_copy(buf, slot).wait_recv()

        @pl.when(has_low)
        def _():
            down_copy(buf, slot).wait_send()
            up_copy(buf, slot).wait_recv()

    def zero_edges(buf):
        @pl.when(tile == 0)
        def _():
            buf[pl.ds(0, halo)] = jnp.zeros((halo,) + buf.shape[1:], jnp.float32)

        @pl.when(tile == tile_count - 1)
        def _():
            buf[pl.ds(halo + height, halo)] = jnp.zeros((halo,) + buf.shape[1:], jnp.float32)

    def to_rows(flat, buf, vregs):
        for r in range(height):
            for b in range(vregs):
                buf[halo + r, b] = flat[pl.ds(b * SUB * height + r, SUB, stride=height), :]

    def from_rows(buf, flat, vregs):
        for r in range(height):
            for b in range(vregs):
                flat[pl.ds(b * SUB * height + r, SUB, stride=height), :] = buf[halo + r, b]

    coef_flat[...] = jnp.zeros(coef_flat.shape, jnp.float32)
    coef_flat[0 : 2 * height, :] = loc_coef[...]
    coef_flat[2 * height : 4 * height, :] = static_coef[...]
    for r in range(height):
        coef_rows[halo + r] = coef_flat[pl.ds(r, SUB, stride=height), :]
    to_rows(alpha, field_a, alpha_vregs)
    for buf in (field_a, field_b, field_s, field_g):
        zero_edges(buf)
    zero_edges(coef_rows)

    pl.semaphore_wait(barrier, chips + has_low.astype(jnp.int32) + has_high.astype(jnp.int32))

    halo_start(coef_rows, 0)
    halo_start(field_a, 1)

    for load in loads:
        load.wait()
    static_flat[...] = jnp.zeros(static_flat.shape, jnp.float32)
    static_flat[0 : fields * height, :] = own_ctl[...].reshape(fields * height, LANES)
    to_rows(static_flat, field_s, static_vregs)
    halo_start(field_s, 2)

    padded = static_vregs * SUB
    matrix[...] = jnp.zeros(matrix.shape, jnp.float32)
    mask = obs_mask[...].astype(jnp.float32)
    for v in range(variables):
        for l in range(share):
            f = v * share + l
            scaled = mask * own_weight[v, l]
            matrix[f : f + 1, :] = scaled
            matrix[padded + f : padded + f + 1, :] = scaled * own_value[v, l]
    whole = matrix[...]
    coarse = whole.astype(jnp.bfloat16).astype(jnp.float32)
    both = jnp.concatenate([coarse, whole - coarse], axis=0).astype(jnp.bfloat16)

    def cells(r, carry):
        number = lax.broadcasted_iota(jnp.int32, (LANES, stations), 0) + r * LANES
        hot = jnp.where(number == obs_cell[...], 1.0, 0.0).astype(jnp.bfloat16)
        sums = lax.dot_general(
            both, hot, (((1,), (1,)), ((), ())), preferred_element_type=jnp.float32
        )
        total = sums[: 2 * padded] + sums[2 * padded :]
        obs_scale[r] = total[:padded].reshape(static_vregs, SUB, LANES)
        obs_shift[r] = total[padded:].reshape(static_vregs, SUB, LANES)
        return carry

    lax.fori_loop(0, height, cells, 0)

    halo_wait(coef_rows, 0)
    extent = height * tile_count
    lane = lax.broadcasted_iota(jnp.int32, (SUB, SUB, LANES), 2)
    for which, coefs in ((0, coef_loc), (1, coef_static)):
        center, down, right, left = coefs.at[0], coefs.at[1], coefs.at[2], coefs.at[3]
        total_rows = 2 * halo + height
        shape = (SUB, SUB, LANES)
        for start in range(0, total_rows, SUB):
            position = lax.broadcasted_iota(jnp.int32, shape, 0) + (tile * height - halo + start)
            inside = (position >= 0) & (position < extent)
            x = jnp.broadcast_to(coef_rows[start : start + SUB, 2 * which : 2 * which + 1, :], shape)
            y = jnp.broadcast_to(
                coef_rows[start : start + SUB, 2 * which + 1 : 2 * which + 2, :], shape
            )
            if start == 0:
                before = jnp.concatenate([x[:1], x[:-1]], axis=0)
            else:
                before = jnp.broadcast_to(
                    coef_rows[start - 1 : start - 1 + SUB, 2 * which : 2 * which + 1, :], shape
                )
            before = jnp.where(position >= 1, before, 0.0)
            y_left = jnp.where(lane > 0, pltpu.roll(y, 1, 2), 0.0)
            down[start : start + SUB, 0] = jnp.where(
                (position >= 0) & (position < extent - 1), x, 0.0
            )
            center[start : start + SUB, 0] = jnp.where(
                inside, 1.0 - (x + before) - (y + y_left), 0.0
            )
            right[start : start + SUB, 0] = jnp.where(inside & (lane < LANES - 1), y, 0.0)
            left[start : start + SUB, 0] = jnp.where(inside, y_left, 0.0)
    loc_set = [coef_loc.at[n] for n in range(4)]
    static_set = [coef_static.at[n] for n in range(4)]

    halo_wait(field_a, 1)
    result = diffuse(field_a, (ping_a0, ping_a1), loc_set, height, 2)
    from_rows(result, local_flat, alpha_vregs)

    def ensemble(owner):
        offset = pl.multiple_of(owner * span, span)
        total = None
        for m in range(members):
            base = pl.multiple_of(m * levels * height + owner * span, span)
            field = local_flat[pl.ds(base, span), :]
            term = field[None] * perturb[m, :, pl.ds(offset, span), :].astype(jnp.float32)
            total = term if total is None else total + term
        return total

    def pair_copy(k):
        return pltpu.make_async_remote_copy(
            src_ref=part_pair.at[k],
            dst_ref=pair_in.at[k],
            send_sem=pair_send.at[k],
            recv_sem=pair_recv.at[k],
            device_id={"mem": partner},
        )

    def chip_copy(k):
        return pltpu.make_async_remote_copy(
            src_ref=part_own.at[k],
            dst_ref=chip_in.at[k],
            send_sem=chip_send.at[k],
            recv_sem=chip_recv.at[k],
            device_id={"mem": lax.rem(chip + k, chips) * 2 + core},
        )

    order = list(range(1, chips)) + [0]
    for k in order:
        owner_chip = lax.rem(chip + k, chips)
        part_pair[k] = ensemble(owner_chip * 2 + (1 - core))
        pair_copy(k).start()
    for k in order:
        owner_chip = lax.rem(chip + k, chips)
        mine = ensemble(owner_chip * 2 + core)
        pair_copy(k).wait_recv()
        part_own[k] = mine + pair_in[k]
        if k > 0:
            chip_copy(k).start()

    halo_wait(field_s, 2)
    static_part = diffuse(field_s, (ping_s0, ping_s1), static_set, height, 4)
    for k in order:
        pair_copy(k).wait_send()
    total = part_own[0]
    for k in range(1, chips):
        chip_copy(k).wait_recv()
        total = total + chip_in[k]
    static_flat[0 : fields * height, :] = total.reshape(fields * height, LANES)
    for r in range(height):
        for b in range(static_vregs):
            at = pl.ds(b * SUB * height + r, SUB, stride=height)
            increment = static_flat[at, :] + static_part[halo + r, b]
            field_g[halo + r, b] = obs_scale[r, b] * increment - obs_shift[r, b]
    halo_start(field_g, 3)
    from_rows(field_g, static_flat, static_vregs)
    grads[0, 0] = static_flat[0 : fields * height, :].reshape(variables, span, LANES)

    def gather_copy(k):
        return pltpu.make_async_remote_copy(
            src_ref=grads.at[0, 0],
            dst_ref=grads.at[0, k],
            send_sem=gather_send.at[k],
            recv_sem=gather_recv.at[k],
            device_id={"mem": lax.rem(chip + k, chips) * 2 + core},
        )

    def relay_copy(k):
        return pltpu.make_async_remote_copy(
            src_ref=grads.at[0, k],
            dst_ref=grads.at[1, k],
            send_sem=relay_send.at[k],
            recv_sem=relay_recv.at[k],
            device_id={"mem": partner},
        )

    for k in range(1, chips):
        gather_copy(k).start()
    relay_copy(0).start()

    def project(way, k):
        source = lax.rem(chip + chips - k, chips) * 2 + (core if way == 0 else 1 - core)
        offset = pl.multiple_of(source * span, span)
        for m in range(members):
            base = pl.multiple_of(m * levels * height + source * span, span)
            total = None
            for v in range(variables):
                weight = perturb[m, v, pl.ds(offset, span), :].astype(jnp.float32)
                term = weight * grads[way, k, v]
                total = term if total is None else total + term
            local_flat[pl.ds(base, span), :] = total

    project(0, 0)
    halo_wait(field_g, 3)
    result = diffuse(field_g, (ping_s0, ping_s1), static_set, height, 4)
    from_rows(result, static_flat, static_vregs)
    out_static[...] = static_flat[0 : fields * height, :]

    for k in range(1, chips):
        gather_copy(k).wait_recv()
        relay_copy(k).start()
        project(0, k)
    for k in range(chips):
        relay_copy(k).wait_recv()
        project(1, k)
    to_rows(local_flat, field_b, alpha_vregs)
    halo_start(field_b, 4)
    for k in range(1, chips):
        chip_copy(k).wait_send()
        gather_copy(k).wait_send()
    for k in range(chips):
        relay_copy(k).wait_send()
    halo_wait(field_b, 4)
    result = diffuse(field_b, (ping_a0, ping_a1), loc_set, height, 2)
    from_rows(result, out_alpha, alpha_vregs)


def local(
    perturb,
    alpha,
    alpha_mom,
    static_ctl,
    static_mom,
    loc_coef,
    static_coef,
    obs_cell,
    obs_mask,
    obs_value,
    obs_weight,
):
    mem_count = lax.axis_size("mem")
    tile_count = lax.axis_size("tile")
    members, variables, levels, height, width = perturb.shape
    stations = obs_cell.shape[1]
    chips = mem_count // 2
    share = levels // mem_count
    fields = variables * share
    span = share * height
    alpha_vregs = members * levels // SUB
    static_vregs = -(-fields // SUB)
    rows = 2 * DIFF_STEPS + height + 4
    dims = (mem_count, tile_count, members, variables, levels, height, stations)
    f32 = jnp.float32
    vmem = pl.BlockSpec(memory_space=pltpu.VMEM)
    anywhere = pl.BlockSpec(memory_space=pl.ANY)
    dma = pltpu.SemaphoreType.DMA
    chunk = (chips, variables, span, width)
    alpha_smooth, static_smooth = pl.pallas_call(
        functools.partial(kernel, dims),
        out_shape=(
            jax.ShapeDtypeStruct((members * levels * height, width), f32),
            jax.ShapeDtypeStruct((fields * height, width), f32),
        ),
        in_specs=[vmem] * 6 + [anywhere] * 3,
        out_specs=(vmem, vmem),
        scratch_shapes=[
            pltpu.VMEM((rows, alpha_vregs, SUB, width), f32),
            pltpu.VMEM((rows, alpha_vregs, SUB, width), f32),
            pltpu.VMEM((rows, alpha_vregs, SUB, width), f32),
            pltpu.VMEM((rows, alpha_vregs, SUB, width), f32),
            pltpu.VMEM((rows, static_vregs, SUB, width), f32),
            pltpu.VMEM((rows, static_vregs, SUB, width), f32),
            pltpu.VMEM((rows, static_vregs, SUB, width), f32),
            pltpu.VMEM((rows, static_vregs, SUB, width), f32),
            pltpu.VMEM((SUB * height, width), f32),
            pltpu.VMEM((rows, SUB, width), f32),
            pltpu.VMEM((4, rows, 1, SUB, width), f32),
            pltpu.VMEM((4, rows, 1, SUB, width), f32),
            pltpu.VMEM((variables, share, height, width), f32),
            pltpu.VMEM((variables, share, 1, stations), f32),
            pltpu.VMEM((variables, share, 1, stations), f32),
            pltpu.VMEM((2 * static_vregs * SUB, stations), f32),
            pltpu.VMEM((height, static_vregs, SUB, width), f32),
            pltpu.VMEM((height, static_vregs, SUB, width), f32),
            pltpu.VMEM((static_vregs * SUB * height, width), f32),
            pltpu.VMEM((members * levels * height, width), f32),
            pltpu.VMEM(chunk, f32),
            pltpu.VMEM(chunk, f32),
            pltpu.VMEM(chunk, f32),
            pltpu.VMEM(chunk, f32),
            pltpu.VMEM((2,) + chunk, f32),
            dma((3,)),
            dma((5, 2)),
            dma((5, 2)),
            dma((chips,)),
            dma((chips,)),
            dma((chips,)),
            dma((chips,)),
            dma((chips,)),
            dma((chips,)),
            dma((chips,)),
            dma((chips,)),
        ],
        compiler_params=pltpu.CompilerParams(
            collective_id=0, has_side_effects=True, vmem_limit_bytes=48 * 1024 * 1024
        ),
        name="analysis",
    )(
        perturb.reshape(members, variables, levels * height, width),
        alpha.reshape(members * levels * height, width),
        loc_coef.reshape(2 * height, width),
        static_coef.reshape(2 * height, width),
        obs_cell,
        obs_mask,
        static_ctl,
        obs_value,
        obs_weight,
    )
    own_ctl = lax.dynamic_slice_in_dim(static_ctl, lax.axis_index("mem") * share, share, 1)
    alpha_grad = alpha + alpha_smooth.reshape(alpha.shape)
    static_grad = own_ctl + static_smooth.reshape(own_ctl.shape)
    new_alpha_mom = momentum_rate * alpha_mom + alpha_grad
    new_alpha = alpha - step_rate * new_alpha_mom
    new_static_mom = momentum_rate * static_mom + static_grad
    new_static = own_ctl - step_rate * new_static_mom
    return (new_alpha, new_alpha_mom, new_static, new_static_mom)


def solution(mesh):
    return jax.shard_map(
        local,
        mesh=mesh,
        in_specs=(
            P("mem", None, None, "tile", None),
            P("mem", None, "tile", None),
            P("mem", None, "tile", None),
            P(None, None, "tile", None),
            P(None, "mem", "tile", None),
            P(None, "tile", None),
            P(None, "tile", None),
            P("tile", None),
            P("tile", None),
            P(None, None, "tile", None),
            P(None, None, "tile", None),
        ),
        out_specs=(
            P("mem", None, "tile", None),
            P("mem", None, "tile", None),
            P(None, "mem", "tile", None),
            P(None, "mem", "tile", None),
        ),
        check_vma=False,
    )
```

```python
import functools

import jax
import jax.numpy as jnp
from jax import lax
from jax.experimental import pallas as pl
from jax.experimental.pallas import tpu as pltpu
from jax.sharding import PartitionSpec as P

DIFF_STEPS = 12
LANES = 128
SUB = 8

momentum_rate = 0.9
step_rate = 0.5


def diffuse(src, bufs, coefs, height, block):
    center, down, right, left = coefs
    current = src
    for turn in range(DIFF_STEPS):
        target = bufs[turn % 2]
        low = turn + 1
        count = height + 2 * (DIFF_STEPS - 1 - turn)

        def rows(b, carry, current=current, target=target, low=low):
            i = low + b * block
            window = current[pl.ds(i - 1, block + 2)]
            faces = down[pl.ds(i - 1, block + 1)]
            f = window[1 : block + 1]
            new = center[pl.ds(i, block)] * f
            new = new + (faces[1:] * window[2:] + faces[:-1] * window[:-2])
            new = new + (
                right[pl.ds(i, block)] * pltpu.roll(f, LANES - 1, 3)
                + left[pl.ds(i, block)] * pltpu.roll(f, 1, 3)
            )
            target[pl.ds(i, block)] = new
            return carry

        lax.fori_loop(0, -(-count // block), rows, 0, unroll=True)
        current = target
    return current


def kernel(
    dims,
    perturb_hbm,
    alpha_hbm,
    loc_hbm,
    coef_hbm,
    cell_hbm,
    mask_hbm,
    static_hbm,
    value_hbm,
    weight_hbm,
    out_alpha,
    out_static,
    alpha,
    own_ctl,
    perturb,
    obs_cell,
    obs_mask,
    field_a,
    field_b,
    ping_a0,
    ping_a1,
    field_s,
    field_g,
    ping_s0,
    ping_s1,
    coef_flat,
    coef_rows,
    coef_loc,
    coef_static,
    own_value,
    own_weight,
    matrix,
    obs_scale,
    obs_shift,
    static_flat,
    local_flat,
    part_own,
    part_pair,
    pair_in,
    chip_in,
    grads,
    load_sem,
    halo_send,
    halo_recv,
    pair_send,
    pair_recv,
    chip_send,
    chip_recv,
    gather_send,
    gather_recv,
    relay_send,
    relay_recv,
):
    mem_count, tile_count, members, variables, levels, height, stations = dims
    chips = mem_count // 2
    share = levels // mem_count
    fields = variables * share
    span = share * height
    static_vregs = field_s.shape[1]
    alpha_vregs = field_a.shape[1]
    mem = lax.axis_index("mem")
    tile = lax.axis_index("tile")
    chip = mem // 2
    core = lax.rem(mem, 2)
    partner = chip * 2 + (1 - core)
    first = mem * share
    halo = DIFF_STEPS
    has_low = tile > 0
    has_high = tile < tile_count - 1

    sources = [
        (loc_hbm, coef_flat.at[pl.ds(0, 2 * height)]),
        (coef_hbm, coef_flat.at[pl.ds(2 * height, 2 * height)]),
        (alpha_hbm, alpha),
        (static_hbm.at[:, pl.ds(first, share)], own_ctl),
        (cell_hbm, obs_cell),
        (mask_hbm, obs_mask),
        (value_hbm.at[:, pl.ds(first, share)], own_value),
        (weight_hbm.at[:, pl.ds(first, share)], own_weight),
        (perturb_hbm, perturb),
    ]
    loads = [
        pltpu.make_async_copy(source, target, load_sem.at[n])
        for n, (source, target) in enumerate(sources)
    ]
    for load in loads:
        load.start()

    barrier = pltpu.get_barrier_semaphore()
    pl.semaphore_signal(barrier, inc=1, device_id={"mem": partner})
    for k in range(1, chips):
        pl.semaphore_signal(
            barrier, inc=1, device_id={"mem": lax.rem(chip + k, chips) * 2 + core}
        )

    @pl.when(has_low)
    def _():
        pl.semaphore_signal(barrier, inc=1, device_id={"tile": tile - 1})

    @pl.when(has_high)
    def _():
        pl.semaphore_signal(barrier, inc=1, device_id={"tile": tile + 1})

    def up_copy(buf, slot):
        return pltpu.make_async_remote_copy(
            src_ref=buf.at[pl.ds(height, halo)],
            dst_ref=buf.at[pl.ds(0, halo)],
            send_sem=halo_send.at[slot, 0],
            recv_sem=halo_recv.at[slot, 0],
            device_id={"tile": tile + 1},
        )

    def down_copy(buf, slot):
        return pltpu.make_async_remote_copy(
            src_ref=buf.at[pl.ds(halo, halo)],
            dst_ref=buf.at[pl.ds(halo + height, halo)],
            send_sem=halo_send.at[slot, 1],
            recv_sem=halo_recv.at[slot, 1],
            device_id={"tile": tile - 1},
        )

    def halo_start(buf, slot):
        @pl.when(has_high)
        def _():
            up_copy(buf, slot).start()

        @pl.when(has_low)
        def _():
            down_copy(buf, slot).start()

    def halo_wait(buf, slot):
        @pl.when(has_high)
        def _():
            up_copy(buf, slot).wait_send()
            down_copy(buf, slot).wait_recv()

        @pl.when(has_low)
        def _():
            down_copy(buf, slot).wait_send()
            up_copy(buf, slot).wait_recv()

    def zero_edges(buf):
        @pl.when(tile == 0)
        def _():
            buf[pl.ds(0, halo)] = jnp.zeros((halo,) + buf.shape[1:], jnp.float32)

        @pl.when(tile == tile_count - 1)
        def _():
            buf[pl.ds(halo + height, halo)] = jnp.zeros((halo,) + buf.shape[1:], jnp.float32)

    def to_rows(flat, buf, vregs):
        for r in range(height):
            for b in range(vregs):
                buf[halo + r, b] = flat[pl.ds(b * SUB * height + r, SUB, stride=height), :]

    def from_rows(buf, flat, vregs):
        for r in range(height):
            for b in range(vregs):
                flat[pl.ds(b * SUB * height + r, SUB, stride=height), :] = buf[halo + r, b]

    coef_flat[4 * height :, :] = jnp.zeros((4 * height, LANES), jnp.float32)
    for load in loads[:3]:
        load.wait()
    for r in range(height):
        coef_rows[halo + r] = coef_flat[pl.ds(r, SUB, stride=height), :]
    to_rows(alpha, field_a, alpha_vregs)
    for buf in (field_a, field_b, field_s, field_g):
        zero_edges(buf)
    zero_edges(coef_rows)

    pl.semaphore_wait(barrier, chips + has_low.astype(jnp.int32) + has_high.astype(jnp.int32))

    halo_start(coef_rows, 0)
    halo_start(field_a, 1)

    loads[3].wait()
    static_flat[...] = jnp.zeros(static_flat.shape, jnp.float32)
    static_flat[0 : fields * height, :] = own_ctl[...].reshape(fields * height, LANES)
    to_rows(static_flat, field_s, static_vregs)
    halo_start(field_s, 2)

    for load in loads[4:]:
        load.wait()
    padded = static_vregs * SUB
    matrix[...] = jnp.zeros(matrix.shape, jnp.float32)
    mask = obs_mask[...].astype(jnp.float32)
    for v in range(variables):
        for l in range(share):
            f = v * share + l
            scaled = mask * own_weight[v, l]
            matrix[f : f + 1, :] = scaled
            matrix[padded + f : padded + f + 1, :] = scaled * own_value[v, l]
    whole = matrix[...]
    coarse = whole.astype(jnp.bfloat16).astype(jnp.float32)
    both = jnp.concatenate([coarse, whole - coarse], axis=0).astype(jnp.bfloat16)

    def cells(r, carry):
        number = lax.broadcasted_iota(jnp.int32, (LANES, stations), 0) + r * LANES
        hot = jnp.where(number == obs_cell[...], 1.0, 0.0).astype(jnp.bfloat16)
        sums = lax.dot_general(
            both, hot, (((1,), (1,)), ((), ())), preferred_element_type=jnp.float32
        )
        total = sums[: 2 * padded] + sums[2 * padded :]
        obs_scale[r] = total[:padded].reshape(static_vregs, SUB, LANES)
        obs_shift[r] = total[padded:].reshape(static_vregs, SUB, LANES)
        return carry

    lax.fori_loop(0, height, cells, 0)

    halo_wait(coef_rows, 0)
    extent = height * tile_count
    lane = lax.broadcasted_iota(jnp.int32, (SUB, SUB, LANES), 2)
    for which, coefs in ((0, coef_loc), (1, coef_static)):
        center, down, right, left = coefs.at[0], coefs.at[1], coefs.at[2], coefs.at[3]
        total_rows = 2 * halo + height
        shape = (SUB, SUB, LANES)
        for start in range(0, total_rows, SUB):
            position = lax.broadcasted_iota(jnp.int32, shape, 0) + (tile * height - halo + start)
            inside = (position >= 0) & (position < extent)
            x = jnp.broadcast_to(coef_rows[start : start + SUB, 2 * which : 2 * which + 1, :], shape)
            y = jnp.broadcast_to(
                coef_rows[start : start + SUB, 2 * which + 1 : 2 * which + 2, :], shape
            )
            if start == 0:
                before = jnp.concatenate([x[:1], x[:-1]], axis=0)
            else:
                before = jnp.broadcast_to(
                    coef_rows[start - 1 : start - 1 + SUB, 2 * which : 2 * which + 1, :], shape
                )
            before = jnp.where(position >= 1, before, 0.0)
            y_left = jnp.where(lane > 0, pltpu.roll(y, 1, 2), 0.0)
            down[start : start + SUB, 0] = jnp.where(
                (position >= 0) & (position < extent - 1), x, 0.0
            )
            center[start : start + SUB, 0] = jnp.where(
                inside, 1.0 - (x + before) - (y + y_left), 0.0
            )
            right[start : start + SUB, 0] = jnp.where(inside & (lane < LANES - 1), y, 0.0)
            left[start : start + SUB, 0] = jnp.where(inside, y_left, 0.0)
    loc_set = [coef_loc.at[n] for n in range(4)]
    static_set = [coef_static.at[n] for n in range(4)]

    halo_wait(field_a, 1)
    result = diffuse(field_a, (ping_a0, ping_a1), loc_set, height, 2)
    from_rows(result, local_flat, alpha_vregs)

    def ensemble(owner):
        offset = pl.multiple_of(owner * span, span)
        total = None
        for m in range(members):
            base = pl.multiple_of(m * levels * height + owner * span, span)
            field = local_flat[pl.ds(base, span), :]
            term = field[None] * perturb[m, :, pl.ds(offset, span), :].astype(jnp.float32)
            total = term if total is None else total + term
        return total

    def pair_copy(k):
        return pltpu.make_async_remote_copy(
            src_ref=part_pair.at[k],
            dst_ref=pair_in.at[k],
            send_sem=pair_send.at[k],
            recv_sem=pair_recv.at[k],
            device_id={"mem": partner},
        )

    def chip_copy(k):
        return pltpu.make_async_remote_copy(
            src_ref=part_own.at[k],
            dst_ref=chip_in.at[k],
            send_sem=chip_send.at[k],
            recv_sem=chip_recv.at[k],
            device_id={"mem": lax.rem(chip + k, chips) * 2 + core},
        )

    order = list(range(1, chips)) + [0]
    for k in order:
        owner_chip = lax.rem(chip + k, chips)
        part_pair[k] = ensemble(owner_chip * 2 + (1 - core))
        pair_copy(k).start()
    for k in order:
        owner_chip = lax.rem(chip + k, chips)
        mine = ensemble(owner_chip * 2 + core)
        pair_copy(k).wait_recv()
        part_own[k] = mine + pair_in[k]
        if k > 0:
            chip_copy(k).start()

    halo_wait(field_s, 2)
    static_part = diffuse(field_s, (ping_s0, ping_s1), static_set, height, 4)
    for k in order:
        pair_copy(k).wait_send()
    total = part_own[0]
    for k in range(1, chips):
        chip_copy(k).wait_recv()
        total = total + chip_in[k]
    static_flat[0 : fields * height, :] = total.reshape(fields * height, LANES)
    for r in range(height):
        for b in range(static_vregs):
            at = pl.ds(b * SUB * height + r, SUB, stride=height)
            increment = static_flat[at, :] + static_part[halo + r, b]
            field_g[halo + r, b] = obs_scale[r, b] * increment - obs_shift[r, b]
    halo_start(field_g, 3)
    from_rows(field_g, static_flat, static_vregs)
    grads[0, 0] = static_flat[0 : fields * height, :].reshape(variables, span, LANES)

    def gather_copy(k):
        return pltpu.make_async_remote_copy(
            src_ref=grads.at[0, 0],
            dst_ref=grads.at[0, k],
            send_sem=gather_send.at[k],
            recv_sem=gather_recv.at[k],
            device_id={"mem": lax.rem(chip + k, chips) * 2 + core},
        )

    def relay_copy(k):
        return pltpu.make_async_remote_copy(
            src_ref=grads.at[0, k],
            dst_ref=grads.at[1, k],
            send_sem=relay_send.at[k],
            recv_sem=relay_recv.at[k],
            device_id={"mem": partner},
        )

    for k in range(1, chips):
        gather_copy(k).start()
    relay_copy(0).start()

    def project(way, k):
        source = lax.rem(chip + chips - k, chips) * 2 + (core if way == 0 else 1 - core)
        offset = pl.multiple_of(source * span, span)
        for m in range(members):
            base = pl.multiple_of(m * levels * height + source * span, span)
            total = None
            for v in range(variables):
                weight = perturb[m, v, pl.ds(offset, span), :].astype(jnp.float32)
                term = weight * grads[way, k, v]
                total = term if total is None else total + term
            local_flat[pl.ds(base, span), :] = total

    project(0, 0)
    halo_wait(field_g, 3)
    result = diffuse(field_g, (ping_s0, ping_s1), static_set, height, 4)
    from_rows(result, static_flat, static_vregs)
    out_static[...] = static_flat[0 : fields * height, :]

    for k in range(1, chips):
        gather_copy(k).wait_recv()
        relay_copy(k).start()
        project(0, k)
    for k in range(chips):
        relay_copy(k).wait_recv()
        project(1, k)
    to_rows(local_flat, field_b, alpha_vregs)
    halo_start(field_b, 4)
    for k in range(1, chips):
        chip_copy(k).wait_send()
        gather_copy(k).wait_send()
    for k in range(chips):
        relay_copy(k).wait_send()
    halo_wait(field_b, 4)
    result = diffuse(field_b, (ping_a0, ping_a1), loc_set, height, 2)
    from_rows(result, out_alpha, alpha_vregs)


def local(
    perturb,
    alpha,
    alpha_mom,
    static_ctl,
    static_mom,
    loc_coef,
    static_coef,
    obs_cell,
    obs_mask,
    obs_value,
    obs_weight,
):
    mem_count = lax.axis_size("mem")
    tile_count = lax.axis_size("tile")
    members, variables, levels, height, width = perturb.shape
    stations = obs_cell.shape[1]
    chips = mem_count // 2
    share = levels // mem_count
    fields = variables * share
    span = share * height
    alpha_vregs = members * levels // SUB
    static_vregs = -(-fields // SUB)
    rows = 2 * DIFF_STEPS + height + 4
    dims = (mem_count, tile_count, members, variables, levels, height, stations)
    f32 = jnp.float32
    vmem = pl.BlockSpec(memory_space=pltpu.VMEM)
    in_hbm = pl.BlockSpec(memory_space=pltpu.HBM)
    dma = pltpu.SemaphoreType.DMA
    chunk = (chips, variables, span, width)
    alpha_smooth, static_smooth, alpha_copy, own_ctl = pl.pallas_call(
        functools.partial(kernel, dims),
        out_shape=(
            jax.ShapeDtypeStruct((members * levels * height, width), f32),
            jax.ShapeDtypeStruct((fields * height, width), f32),
            jax.ShapeDtypeStruct((members * levels * height, width), f32),
            jax.ShapeDtypeStruct((variables, share, height, width), f32),
        ),
        in_specs=[in_hbm] * 9,
        out_specs=(vmem,) * 4,
        scratch_shapes=[
            pltpu.VMEM((members, variables, levels * height, width), perturb.dtype),
            pltpu.VMEM(obs_cell.shape, obs_cell.dtype),
            pltpu.VMEM(obs_mask.shape, obs_mask.dtype),
            pltpu.VMEM((rows, alpha_vregs, SUB, width), f32),
            pltpu.VMEM((rows, alpha_vregs, SUB, width), f32),
            pltpu.VMEM((rows, alpha_vregs, SUB, width), f32),
            pltpu.VMEM((rows, alpha_vregs, SUB, width), f32),
            pltpu.VMEM((rows, static_vregs, SUB, width), f32),
            pltpu.VMEM((rows, static_vregs, SUB, width), f32),
            pltpu.VMEM((rows, static_vregs, SUB, width), f32),
            pltpu.VMEM((rows, static_vregs, SUB, width), f32),
            pltpu.VMEM((SUB * height, width), f32),
            pltpu.VMEM((rows, SUB, width), f32),
            pltpu.VMEM((4, rows, 1, SUB, width), f32),
            pltpu.VMEM((4, rows, 1, SUB, width), f32),
            pltpu.VMEM((variables, share, 1, stations), f32),
            pltpu.VMEM((variables, share, 1, stations), f32),
            pltpu.VMEM((2 * static_vregs * SUB, stations), f32),
            pltpu.VMEM((height, static_vregs, SUB, width), f32),
            pltpu.VMEM((height, static_vregs, SUB, width), f32),
            pltpu.VMEM((static_vregs * SUB * height, width), f32),
            pltpu.VMEM((members * levels * height, width), f32),
            pltpu.VMEM(chunk, f32),
            pltpu.VMEM(chunk, f32),
            pltpu.VMEM(chunk, f32),
            pltpu.VMEM(chunk, f32),
            pltpu.VMEM((2,) + chunk, f32),
            dma((9,)),
            dma((5, 2)),
            dma((5, 2)),
            dma((chips,)),
            dma((chips,)),
            dma((chips,)),
            dma((chips,)),
            dma((chips,)),
            dma((chips,)),
            dma((chips,)),
            dma((chips,)),
        ],
        compiler_params=pltpu.CompilerParams(
            collective_id=0, has_side_effects=True, vmem_limit_bytes=60 * 1024 * 1024
        ),
        name="analysis",
    )(
        perturb.reshape(members, variables, levels * height, width),
        alpha.reshape(members * levels * height, width),
        loc_coef.reshape(2 * height, width),
        static_coef.reshape(2 * height, width),
        obs_cell,
        obs_mask,
        static_ctl,
        obs_value,
        obs_weight,
    )
    alpha = alpha_copy.reshape(alpha.shape)
    alpha_grad = alpha + alpha_smooth.reshape(alpha.shape)
    static_grad = own_ctl + static_smooth.reshape(own_ctl.shape)
    new_alpha_mom = momentum_rate * alpha_mom + alpha_grad
    new_alpha = alpha - step_rate * new_alpha_mom
    new_static_mom = momentum_rate * static_mom + static_grad
    new_static = own_ctl - step_rate * new_static_mom
    return (new_alpha, new_alpha_mom, new_static, new_static_mom)


def solution(mesh):
    return jax.shard_map(
        local,
        mesh=mesh,
        in_specs=(
            P("mem", None, None, "tile", None),
            P("mem", None, "tile", None),
            P("mem", None, "tile", None),
            P(None, None, "tile", None),
            P(None, "mem", "tile", None),
            P(None, "tile", None),
            P(None, "tile", None),
            P("tile", None),
            P("tile", None),
            P(None, None, "tile", None),
            P(None, None, "tile", None),
        ),
        out_specs=(
            P("mem", None, "tile", None),
            P("mem", None, "tile", None),
            P(None, "mem", "tile", None),
            P(None, "mem", "tile", None),
        ),
        check_vma=False,
    )
```

```python
import functools

import jax
import jax.numpy as jnp
from jax import lax
from jax.experimental import pallas as pl
from jax.experimental.pallas import tpu as pltpu
from jax.sharding import PartitionSpec as P

DIFF_STEPS = 12
LANES = 128
SUB = 8

momentum_rate = 0.9
step_rate = 0.5


def diffuse(src, bufs, coefs, height, block):
    center, down, right, left = coefs
    current = src
    for turn in range(DIFF_STEPS):
        target = bufs[turn % 2]
        low = turn + 1
        count = height + 2 * (DIFF_STEPS - 1 - turn)

        def rows(b, carry, current=current, target=target, low=low):
            i = low + b * block
            window = current[pl.ds(i - 1, block + 2)]
            faces = down[pl.ds(i - 1, block + 1)]
            f = window[1 : block + 1]
            new = center[pl.ds(i, block)] * f
            new = new + (faces[1:] * window[2:] + faces[:-1] * window[:-2])
            new = new + (
                right[pl.ds(i, block)] * pltpu.roll(f, LANES - 1, 3)
                + left[pl.ds(i, block)] * pltpu.roll(f, 1, 3)
            )
            target[pl.ds(i, block)] = new
            return carry

        lax.fori_loop(0, -(-count // block), rows, 0, unroll=True)
        current = target
    return current


def kernel(
    dims,
    perturb_hbm,
    alpha_hbm,
    loc_hbm,
    coef_hbm,
    cell_hbm,
    mask_hbm,
    static_hbm,
    value_hbm,
    weight_hbm,
    out_alpha,
    out_static,
    own_ctl,
    alpha,
    perturb,
    obs_cell,
    obs_mask,
    field_a,
    field_b,
    ping_a0,
    ping_a1,
    field_s,
    field_g,
    ping_s0,
    ping_s1,
    coef_flat,
    coef_rows,
    coef_loc,
    coef_static,
    own_value,
    own_weight,
    matrix,
    obs_scale,
    obs_shift,
    static_flat,
    local_flat,
    part_own,
    part_pair,
    pair_in,
    chip_in,
    grads,
    load_sem,
    halo_send,
    halo_recv,
    pair_send,
    pair_recv,
    chip_send,
    chip_recv,
    gather_send,
    gather_recv,
    relay_send,
    relay_recv,
):
    mem_count, tile_count, members, variables, levels, height, stations = dims
    chips = mem_count // 2
    share = levels // mem_count
    fields = variables * share
    span = share * height
    static_vregs = field_s.shape[1]
    alpha_vregs = field_a.shape[0]
    mem = lax.axis_index("mem")
    tile = lax.axis_index("tile")
    chip = mem // 2
    core = lax.rem(mem, 2)
    partner = chip * 2 + (1 - core)
    first = mem * share
    halo = DIFF_STEPS
    has_low = tile > 0
    has_high = tile < tile_count - 1

    sources = [
        (loc_hbm, coef_flat.at[pl.ds(0, 2 * height)]),
        (coef_hbm, coef_flat.at[pl.ds(2 * height, 2 * height)]),
        (alpha_hbm, alpha),
        (static_hbm.at[:, pl.ds(first, share)], own_ctl),
        (cell_hbm, obs_cell),
        (mask_hbm, obs_mask),
        (value_hbm.at[:, pl.ds(first, share)], own_value),
        (weight_hbm.at[:, pl.ds(first, share)], own_weight),
        (perturb_hbm, perturb),
    ]
    loads = [
        pltpu.make_async_copy(source, target, load_sem.at[n])
        for n, (source, target) in enumerate(sources)
    ]
    for load in loads:
        load.start()

    barrier = pltpu.get_barrier_semaphore()
    pl.semaphore_signal(barrier, inc=1, device_id={"mem": partner})
    for k in range(1, chips):
        pl.semaphore_signal(
            barrier, inc=1, device_id={"mem": lax.rem(chip + k, chips) * 2 + core}
        )

    @pl.when(has_low)
    def _():
        pl.semaphore_signal(barrier, inc=1, device_id={"tile": tile - 1})

    @pl.when(has_high)
    def _():
        pl.semaphore_signal(barrier, inc=1, device_id={"tile": tile + 1})

    def up_copy(buf, slot):
        return pltpu.make_async_remote_copy(
            src_ref=buf.at[pl.ds(height, halo)],
            dst_ref=buf.at[pl.ds(0, halo)],
            send_sem=halo_send.at[slot, 0],
            recv_sem=halo_recv.at[slot, 0],
            device_id={"tile": tile + 1},
        )

    def down_copy(buf, slot):
        return pltpu.make_async_remote_copy(
            src_ref=buf.at[pl.ds(halo, halo)],
            dst_ref=buf.at[pl.ds(halo + height, halo)],
            send_sem=halo_send.at[slot, 1],
            recv_sem=halo_recv.at[slot, 1],
            device_id={"tile": tile - 1},
        )

    def halo_start(buf, slot):
        @pl.when(has_high)
        def _():
            up_copy(buf, slot).start()

        @pl.when(has_low)
        def _():
            down_copy(buf, slot).start()

    def halo_wait(buf, slot):
        @pl.when(has_high)
        def _():
            up_copy(buf, slot).wait_send()
            down_copy(buf, slot).wait_recv()

        @pl.when(has_low)
        def _():
            down_copy(buf, slot).wait_send()
            up_copy(buf, slot).wait_recv()

    def zero_edges(buf):
        @pl.when(tile == 0)
        def _():
            buf[pl.ds(0, halo)] = jnp.zeros((halo,) + buf.shape[1:], jnp.float32)

        @pl.when(tile == tile_count - 1)
        def _():
            buf[pl.ds(halo + height, halo)] = jnp.zeros((halo,) + buf.shape[1:], jnp.float32)

    def to_rows(flat, buf, vregs):
        for r in range(height):
            for b in range(vregs):
                buf[halo + r, b] = flat[pl.ds(b * SUB * height + r, SUB, stride=height), :]

    def from_rows(buf, flat, vregs):
        for r in range(height):
            for b in range(vregs):
                flat[pl.ds(b * SUB * height + r, SUB, stride=height), :] = buf[halo + r, b]

    coef_flat[4 * height :, :] = jnp.zeros((4 * height, LANES), jnp.float32)
    for load in loads[:3]:
        load.wait()
    for r in range(height):
        coef_rows[halo + r] = coef_flat[pl.ds(r, SUB, stride=height), :]
    group_rows = SUB * height
    groups_a = [field_a.at[g] for g in range(alpha_vregs)]
    groups_b = [field_b.at[g] for g in range(alpha_vregs)]

    def group_in(flat, g):
        for r in range(height):
            field = flat[pl.ds(g * group_rows + r, SUB, stride=height), :]
            (field_a if flat is alpha else field_b)[g, halo + r, 0] = field

    def group_out(result, flat, g):
        for r in range(height):
            flat[pl.ds(g * group_rows + r, SUB, stride=height), :] = result[halo + r, 0]

    for g in range(alpha_vregs):
        group_in(alpha, g)
    for buf in groups_a + groups_b + [field_s, field_g]:
        zero_edges(buf)
    zero_edges(coef_rows)

    pl.semaphore_wait(barrier, chips + has_low.astype(jnp.int32) + has_high.astype(jnp.int32))

    halo_start(coef_rows, 0)
    for g in range(alpha_vregs):
        halo_start(groups_a[g], 4 + g)

    loads[3].wait()
    static_flat[...] = jnp.zeros(static_flat.shape, jnp.float32)
    static_flat[0 : fields * height, :] = own_ctl[...].reshape(fields * height, LANES)
    to_rows(static_flat, field_s, static_vregs)
    halo_start(field_s, 2)

    for load in loads[4:]:
        load.wait()
    padded = static_vregs * SUB
    matrix[...] = jnp.zeros(matrix.shape, jnp.float32)
    mask = obs_mask[...].astype(jnp.float32)
    for v in range(variables):
        for l in range(share):
            f = v * share + l
            scaled = mask * own_weight[v, l]
            matrix[f : f + 1, :] = scaled
            matrix[padded + f : padded + f + 1, :] = scaled * own_value[v, l]
    whole = matrix[...]
    coarse = whole.astype(jnp.bfloat16).astype(jnp.float32)
    both = jnp.concatenate([coarse, whole - coarse], axis=0).astype(jnp.bfloat16)

    def cells(r, carry):
        number = lax.broadcasted_iota(jnp.int32, (LANES, stations), 0) + r * LANES
        hot = jnp.where(number == obs_cell[...], 1.0, 0.0).astype(jnp.bfloat16)
        sums = lax.dot_general(
            both, hot, (((1,), (1,)), ((), ())), preferred_element_type=jnp.float32
        )
        total = sums[: 2 * padded] + sums[2 * padded :]
        obs_scale[r] = total[:padded].reshape(static_vregs, SUB, LANES)
        obs_shift[r] = total[padded:].reshape(static_vregs, SUB, LANES)
        return carry

    lax.fori_loop(0, height // 2, cells, 0)

    halo_wait(coef_rows, 0)
    extent = height * tile_count
    lane = lax.broadcasted_iota(jnp.int32, (SUB, SUB, LANES), 2)
    for which, coefs in ((0, coef_loc), (1, coef_static)):
        center, down, right, left = coefs.at[0], coefs.at[1], coefs.at[2], coefs.at[3]
        total_rows = 2 * halo + height
        shape = (SUB, SUB, LANES)
        for start in range(0, total_rows, SUB):
            position = lax.broadcasted_iota(jnp.int32, shape, 0) + (tile * height - halo + start)
            inside = (position >= 0) & (position < extent)
            x = jnp.broadcast_to(coef_rows[start : start + SUB, 2 * which : 2 * which + 1, :], shape)
            y = jnp.broadcast_to(
                coef_rows[start : start + SUB, 2 * which + 1 : 2 * which + 2, :], shape
            )
            if start == 0:
                before = jnp.concatenate([x[:1], x[:-1]], axis=0)
            else:
                before = jnp.broadcast_to(
                    coef_rows[start - 1 : start - 1 + SUB, 2 * which : 2 * which + 1, :], shape
                )
            before = jnp.where(position >= 1, before, 0.0)
            y_left = jnp.where(lane > 0, pltpu.roll(y, 1, 2), 0.0)
            down[start : start + SUB, 0] = jnp.where(
                (position >= 0) & (position < extent - 1), x, 0.0
            )
            center[start : start + SUB, 0] = jnp.where(
                inside, 1.0 - (x + before) - (y + y_left), 0.0
            )
            right[start : start + SUB, 0] = jnp.where(inside & (lane < LANES - 1), y, 0.0)
            left[start : start + SUB, 0] = jnp.where(inside, y_left, 0.0)
    loc_set = [coef_loc.at[n] for n in range(4)]
    static_set = [coef_static.at[n] for n in range(4)]

    for g in range(alpha_vregs):
        halo_wait(groups_a[g], 4 + g)
        result = diffuse(groups_a[g], (ping_a0, ping_a1), loc_set, height, 4)
        group_out(result, local_flat, g)

    def ensemble(owner):
        offset = pl.multiple_of(owner * span, span)
        total = None
        for m in range(members):
            base = pl.multiple_of(m * levels * height + owner * span, span)
            field = local_flat[pl.ds(base, span), :]
            term = field[None] * perturb[m, :, pl.ds(offset, span), :].astype(jnp.float32)
            total = term if total is None else total + term
        return total

    def pair_copy(k):
        return pltpu.make_async_remote_copy(
            src_ref=part_pair.at[k],
            dst_ref=pair_in.at[k],
            send_sem=pair_send.at[k],
            recv_sem=pair_recv.at[k],
            device_id={"mem": partner},
        )

    def chip_copy(k):
        return pltpu.make_async_remote_copy(
            src_ref=part_own.at[k],
            dst_ref=chip_in.at[k],
            send_sem=chip_send.at[k],
            recv_sem=chip_recv.at[k],
            device_id={"mem": lax.rem(chip + k, chips) * 2 + core},
        )

    order = list(range(1, chips)) + [0]
    for k in order:
        owner_chip = lax.rem(chip + k, chips)
        part_pair[k] = ensemble(owner_chip * 2 + (1 - core))
        pair_copy(k).start()
    for k in order:
        owner_chip = lax.rem(chip + k, chips)
        mine = ensemble(owner_chip * 2 + core)
        pair_copy(k).wait_recv()
        part_own[k] = mine + pair_in[k]
        if k > 0:
            chip_copy(k).start()

    lax.fori_loop(height // 2, height, cells, 0)
    halo_wait(field_s, 2)
    static_part = diffuse(field_s, (ping_s0, ping_s1), static_set, height, 4)
    for k in order:
        pair_copy(k).wait_send()
    total = part_own[0]
    for k in range(1, chips):
        chip_copy(k).wait_recv()
        total = total + chip_in[k]
    static_flat[0 : fields * height, :] = total.reshape(fields * height, LANES)
    for r in range(height):
        for b in range(static_vregs):
            at = pl.ds(b * SUB * height + r, SUB, stride=height)
            increment = static_flat[at, :] + static_part[halo + r, b]
            field_g[halo + r, b] = obs_scale[r, b] * increment - obs_shift[r, b]
    halo_start(field_g, 3)
    from_rows(field_g, static_flat, static_vregs)
    grads[0, 0] = static_flat[0 : fields * height, :].reshape(variables, span, LANES)

    def gather_copy(k):
        return pltpu.make_async_remote_copy(
            src_ref=grads.at[0, 0],
            dst_ref=grads.at[0, k],
            send_sem=gather_send.at[k],
            recv_sem=gather_recv.at[k],
            device_id={"mem": lax.rem(chip + k, chips) * 2 + core},
        )

    def relay_copy(k):
        return pltpu.make_async_remote_copy(
            src_ref=grads.at[0, k],
            dst_ref=grads.at[1, k],
            send_sem=relay_send.at[k],
            recv_sem=relay_recv.at[k],
            device_id={"mem": partner},
        )

    for k in range(1, chips):
        gather_copy(k).start()
    relay_copy(0).start()

    def project(way, k):
        source = lax.rem(chip + chips - k, chips) * 2 + (core if way == 0 else 1 - core)
        offset = pl.multiple_of(source * span, span)
        for m in range(members):
            base = pl.multiple_of(m * levels * height + source * span, span)
            total = None
            for v in range(variables):
                weight = perturb[m, v, pl.ds(offset, span), :].astype(jnp.float32)
                term = weight * grads[way, k, v]
                total = term if total is None else total + term
            local_flat[pl.ds(base, span), :] = total

    project(0, 0)
    halo_wait(field_g, 3)
    result = diffuse(field_g, (ping_s0, ping_s1), static_set, height, 4)
    from_rows(result, static_flat, static_vregs)
    out_static[...] = static_flat[0 : fields * height, :]

    for k in range(1, chips):
        gather_copy(k).wait_recv()
        relay_copy(k).start()
        project(0, k)
    for k in range(chips):
        relay_copy(k).wait_recv()
        project(1, k)
    for g in range(alpha_vregs):
        group_in(local_flat, g)
        halo_start(groups_b[g], 4 + alpha_vregs + g)
    for k in range(1, chips):
        chip_copy(k).wait_send()
        gather_copy(k).wait_send()
    for k in range(chips):
        relay_copy(k).wait_send()
    for g in range(alpha_vregs):
        halo_wait(groups_b[g], 4 + alpha_vregs + g)
        result = diffuse(groups_b[g], (ping_a0, ping_a1), loc_set, height, 4)
        group_out(result, out_alpha, g)


def local(
    perturb,
    alpha,
    alpha_mom,
    static_ctl,
    static_mom,
    loc_coef,
    static_coef,
    obs_cell,
    obs_mask,
    obs_value,
    obs_weight,
):
    mem_count = lax.axis_size("mem")
    tile_count = lax.axis_size("tile")
    members, variables, levels, height, width = perturb.shape
    stations = obs_cell.shape[1]
    chips = mem_count // 2
    share = levels // mem_count
    fields = variables * share
    span = share * height
    alpha_vregs = members * levels // SUB
    static_vregs = -(-fields // SUB)
    rows = 2 * DIFF_STEPS + height + 4
    dims = (mem_count, tile_count, members, variables, levels, height, stations)
    f32 = jnp.float32
    vmem = pl.BlockSpec(memory_space=pltpu.VMEM)
    in_hbm = pl.BlockSpec(memory_space=pltpu.HBM)
    dma = pltpu.SemaphoreType.DMA
    chunk = (chips, variables, span, width)
    alpha_smooth, static_smooth, own_ctl = pl.pallas_call(
        functools.partial(kernel, dims),
        out_shape=(
            jax.ShapeDtypeStruct((members * levels * height, width), f32),
            jax.ShapeDtypeStruct((fields * height, width), f32),
            jax.ShapeDtypeStruct((variables, share, height, width), f32),
        ),
        in_specs=[in_hbm] * 9,
        out_specs=(vmem,) * 3,
        scratch_shapes=[
            pltpu.VMEM((members * levels * height, width), f32),
            pltpu.VMEM((members, variables, levels * height, width), perturb.dtype),
            pltpu.VMEM(obs_cell.shape, obs_cell.dtype),
            pltpu.VMEM(obs_mask.shape, obs_mask.dtype),
            pltpu.VMEM((alpha_vregs, rows, 1, SUB, width), f32),
            pltpu.VMEM((alpha_vregs, rows, 1, SUB, width), f32),
            pltpu.VMEM((rows, 1, SUB, width), f32),
            pltpu.VMEM((rows, 1, SUB, width), f32),
            pltpu.VMEM((rows, static_vregs, SUB, width), f32),
            pltpu.VMEM((rows, static_vregs, SUB, width), f32),
            pltpu.VMEM((rows, static_vregs, SUB, width), f32),
            pltpu.VMEM((rows, static_vregs, SUB, width), f32),
            pltpu.VMEM((SUB * height, width), f32),
            pltpu.VMEM((rows, SUB, width), f32),
            pltpu.VMEM((4, rows, 1, SUB, width), f32),
            pltpu.VMEM((4, rows, 1, SUB, width), f32),
            pltpu.VMEM((variables, share, 1, stations), f32),
            pltpu.VMEM((variables, share, 1, stations), f32),
            pltpu.VMEM((2 * static_vregs * SUB, stations), f32),
            pltpu.VMEM((height, static_vregs, SUB, width), f32),
            pltpu.VMEM((height, static_vregs, SUB, width), f32),
            pltpu.VMEM((static_vregs * SUB * height, width), f32),
            pltpu.VMEM((members * levels * height, width), f32),
            pltpu.VMEM(chunk, f32),
            pltpu.VMEM(chunk, f32),
            pltpu.VMEM(chunk, f32),
            pltpu.VMEM(chunk, f32),
            pltpu.VMEM((2,) + chunk, f32),
            dma((9,)),
            dma((4 + 2 * alpha_vregs, 2)),
            dma((4 + 2 * alpha_vregs, 2)),
            dma((chips,)),
            dma((chips,)),
            dma((chips,)),
            dma((chips,)),
            dma((chips,)),
            dma((chips,)),
            dma((chips,)),
            dma((chips,)),
        ],
        compiler_params=pltpu.CompilerParams(
            collective_id=0, has_side_effects=True, vmem_limit_bytes=60 * 1024 * 1024
        ),
        name="analysis",
    )(
        perturb.reshape(members, variables, levels * height, width),
        alpha.reshape(members * levels * height, width),
        loc_coef.reshape(2 * height, width),
        static_coef.reshape(2 * height, width),
        obs_cell,
        obs_mask,
        static_ctl,
        obs_value,
        obs_weight,
    )
    alpha_grad = alpha + alpha_smooth.reshape(alpha.shape)
    static_grad = own_ctl + static_smooth.reshape(own_ctl.shape)
    new_alpha_mom = momentum_rate * alpha_mom + alpha_grad
    new_alpha = alpha - step_rate * new_alpha_mom
    new_static_mom = momentum_rate * static_mom + static_grad
    new_static = own_ctl - step_rate * new_static_mom
    return (new_alpha, new_alpha_mom, new_static, new_static_mom)


def solution(mesh):
    return jax.shard_map(
        local,
        mesh=mesh,
        in_specs=(
            P("mem", None, None, "tile", None),
            P("mem", None, "tile", None),
            P("mem", None, "tile", None),
            P(None, None, "tile", None),
            P(None, "mem", "tile", None),
            P(None, "tile", None),
            P(None, "tile", None),
            P("tile", None),
            P("tile", None),
            P(None, None, "tile", None),
            P(None, None, "tile", None),
        ),
        out_specs=(
            P("mem", None, "tile", None),
            P("mem", None, "tile", None),
            P(None, "mem", "tile", None),
            P(None, "mem", "tile", None),
        ),
        check_vma=False,
    )
```

```python
import functools

import jax
import jax.numpy as jnp
from jax import lax
from jax.experimental import pallas as pl
from jax.experimental.pallas import tpu as pltpu
from jax.sharding import PartitionSpec as P

DIFF_STEPS = 12
LANES = 128
SUB = 8

momentum_rate = 0.9
step_rate = 0.5


def diffuse(src, bufs, coefs, height, block):
    center, down, right, left = coefs
    current = src
    for turn in range(DIFF_STEPS):
        target = bufs[turn % 2]
        low = turn + 1
        count = height + 2 * (DIFF_STEPS - 1 - turn)

        def rows(b, carry, current=current, target=target, low=low):
            i = low + b * block
            window = current[pl.ds(i - 1, block + 2)]
            faces = down[pl.ds(i - 1, block + 1)]
            f = window[1 : block + 1]
            new = center[pl.ds(i, block)] * f
            new = new + (faces[1:] * window[2:] + faces[:-1] * window[:-2])
            new = new + (
                right[pl.ds(i, block)] * pltpu.roll(f, LANES - 1, 3)
                + left[pl.ds(i, block)] * pltpu.roll(f, 1, 3)
            )
            target[pl.ds(i, block)] = new
            return carry

        lax.fori_loop(0, -(-count // block), rows, 0, unroll=True)
        current = target
    return current


def kernel(
    dims,
    perturb_hbm,
    alpha_hbm,
    loc_hbm,
    coef_hbm,
    cell_hbm,
    mask_hbm,
    static_hbm,
    value_hbm,
    weight_hbm,
    out_alpha,
    out_static,
    own_ctl,
    alpha,
    perturb,
    obs_cell,
    obs_mask,
    field_a,
    field_b,
    ping_a0,
    ping_a1,
    field_s,
    field_g,
    ping_s0,
    ping_s1,
    coef_flat,
    coef_rows,
    coef_loc,
    coef_static,
    own_value,
    own_weight,
    matrix,
    obs_scale,
    obs_shift,
    static_flat,
    local_flat,
    part_own,
    part_pair,
    pair_in,
    chip_in,
    grads,
    load_sem,
    halo_send,
    halo_recv,
    pair_send,
    pair_recv,
    chip_send,
    chip_recv,
    gather_send,
    gather_recv,
    relay_send,
    relay_recv,
):
    mem_count, tile_count, members, variables, levels, height, stations = dims
    chips = mem_count // 2
    share = levels // mem_count
    fields = variables * share
    span = share * height
    static_vregs = field_s.shape[1]
    alpha_vregs = field_a.shape[0]
    mem = lax.axis_index("mem")
    tile = lax.axis_index("tile")
    chip = mem // 2
    core = lax.rem(mem, 2)
    partner = chip * 2 + (1 - core)
    first = mem * share
    halo = DIFF_STEPS
    has_low = tile > 0
    has_high = tile < tile_count - 1

    sources = [
        (loc_hbm, coef_flat.at[pl.ds(0, 2 * height)]),
        (coef_hbm, coef_flat.at[pl.ds(2 * height, 2 * height)]),
        (alpha_hbm, alpha),
        (static_hbm.at[:, pl.ds(first, share)], own_ctl),
        (cell_hbm, obs_cell),
        (mask_hbm, obs_mask),
        (value_hbm.at[:, pl.ds(first, share)], own_value),
        (weight_hbm.at[:, pl.ds(first, share)], own_weight),
        (perturb_hbm, perturb),
    ]
    loads = [
        pltpu.make_async_copy(source, target, load_sem.at[n])
        for n, (source, target) in enumerate(sources)
    ]
    for load in loads:
        load.start()

    barrier = pltpu.get_barrier_semaphore()
    pl.semaphore_signal(barrier, inc=1, device_id={"mem": partner})
    for k in range(1, chips):
        pl.semaphore_signal(
            barrier, inc=1, device_id={"mem": lax.rem(chip + k, chips) * 2 + core}
        )

    @pl.when(has_low)
    def _():
        pl.semaphore_signal(barrier, inc=1, device_id={"tile": tile - 1})

    @pl.when(has_high)
    def _():
        pl.semaphore_signal(barrier, inc=1, device_id={"tile": tile + 1})

    def up_copy(buf, slot):
        return pltpu.make_async_remote_copy(
            src_ref=buf.at[pl.ds(height, halo)],
            dst_ref=buf.at[pl.ds(0, halo)],
            send_sem=halo_send.at[slot, 0],
            recv_sem=halo_recv.at[slot, 0],
            device_id={"tile": tile + 1},
        )

    def down_copy(buf, slot):
        return pltpu.make_async_remote_copy(
            src_ref=buf.at[pl.ds(halo, halo)],
            dst_ref=buf.at[pl.ds(halo + height, halo)],
            send_sem=halo_send.at[slot, 1],
            recv_sem=halo_recv.at[slot, 1],
            device_id={"tile": tile - 1},
        )

    def halo_start(buf, slot):
        @pl.when(has_high)
        def _():
            up_copy(buf, slot).start()

        @pl.when(has_low)
        def _():
            down_copy(buf, slot).start()

    def halo_wait(buf, slot):
        @pl.when(has_high)
        def _():
            up_copy(buf, slot).wait_send()
            down_copy(buf, slot).wait_recv()

        @pl.when(has_low)
        def _():
            down_copy(buf, slot).wait_send()
            up_copy(buf, slot).wait_recv()

    def zero_edges(buf):
        @pl.when(tile == 0)
        def _():
            buf[pl.ds(0, halo)] = jnp.zeros((halo,) + buf.shape[1:], jnp.float32)

        @pl.when(tile == tile_count - 1)
        def _():
            buf[pl.ds(halo + height, halo)] = jnp.zeros((halo,) + buf.shape[1:], jnp.float32)

    def to_rows(flat, buf, vregs):
        for r in range(height):
            for b in range(vregs):
                buf[halo + r, b] = flat[pl.ds(b * SUB * height + r, SUB, stride=height), :]

    def from_rows(buf, flat, vregs):
        for r in range(height):
            for b in range(vregs):
                flat[pl.ds(b * SUB * height + r, SUB, stride=height), :] = buf[halo + r, b]

    coef_flat[4 * height :, :] = jnp.zeros((4 * height, LANES), jnp.float32)
    for load in loads[:3]:
        load.wait()
    for r in range(height):
        coef_rows[halo + r] = coef_flat[pl.ds(r, SUB, stride=height), :]
    group_rows = SUB * height
    groups_a = [field_a.at[g] for g in range(alpha_vregs)]
    groups_b = [field_b.at[g] for g in range(alpha_vregs)]

    def group_in(flat, g):
        for r in range(height):
            field = flat[pl.ds(g * group_rows + r, SUB, stride=height), :]
            (field_a if flat is alpha else field_b)[g, halo + r, 0] = field

    def group_out(result, flat, g):
        for r in range(height):
            flat[pl.ds(g * group_rows + r, SUB, stride=height), :] = result[halo + r, 0]

    for g in range(alpha_vregs):
        group_in(alpha, g)
    for buf in groups_a + groups_b + [field_s, field_g]:
        zero_edges(buf)
    zero_edges(coef_rows)

    pl.semaphore_wait(barrier, chips + has_low.astype(jnp.int32) + has_high.astype(jnp.int32))

    halo_start(coef_rows, 0)
    for g in range(alpha_vregs):
        halo_start(groups_a[g], 4 + g)

    loads[3].wait()
    static_flat[...] = jnp.zeros(static_flat.shape, jnp.float32)
    static_flat[0 : fields * height, :] = own_ctl[...].reshape(fields * height, LANES)
    to_rows(static_flat, field_s, static_vregs)
    halo_start(field_s, 2)

    for load in loads[4:]:
        load.wait()
    padded = static_vregs * SUB
    matrix[...] = jnp.zeros(matrix.shape, jnp.float32)
    mask = obs_mask[...].astype(jnp.float32)
    for v in range(variables):
        for l in range(share):
            f = v * share + l
            scaled = mask * own_weight[v, l]
            matrix[f : f + 1, :] = scaled
            matrix[padded + f : padded + f + 1, :] = scaled * own_value[v, l]
    whole = matrix[...]
    coarse = whole.astype(jnp.bfloat16).astype(jnp.float32)
    both = jnp.concatenate([coarse, whole - coarse], axis=0).astype(jnp.bfloat16)

    def cells(r, carry):
        number = lax.broadcasted_iota(jnp.int32, (LANES, stations), 0) + r * LANES
        hot = jnp.where(number == obs_cell[...], 1.0, 0.0).astype(jnp.bfloat16)
        sums = lax.dot_general(
            both, hot, (((1,), (1,)), ((), ())), preferred_element_type=jnp.float32
        )
        total = sums[: 2 * padded] + sums[2 * padded :]
        obs_scale[r] = total[:padded].reshape(static_vregs, SUB, LANES)
        obs_shift[r] = total[padded:].reshape(static_vregs, SUB, LANES)
        return carry

    lax.fori_loop(0, height // 2, cells, 0)

    halo_wait(coef_rows, 0)
    extent = height * tile_count
    lane = lax.broadcasted_iota(jnp.int32, (SUB, SUB, LANES), 2)
    for which, coefs in ((0, coef_loc), (1, coef_static)):
        center, down, right, left = coefs.at[0], coefs.at[1], coefs.at[2], coefs.at[3]
        total_rows = 2 * halo + height
        shape = (SUB, SUB, LANES)
        for start in range(0, total_rows, SUB):
            position = lax.broadcasted_iota(jnp.int32, shape, 0) + (tile * height - halo + start)
            inside = (position >= 0) & (position < extent)
            x = jnp.broadcast_to(coef_rows[start : start + SUB, 2 * which : 2 * which + 1, :], shape)
            y = jnp.broadcast_to(
                coef_rows[start : start + SUB, 2 * which + 1 : 2 * which + 2, :], shape
            )
            if start == 0:
                before = jnp.concatenate([x[:1], x[:-1]], axis=0)
            else:
                before = jnp.broadcast_to(
                    coef_rows[start - 1 : start - 1 + SUB, 2 * which : 2 * which + 1, :], shape
                )
            before = jnp.where(position >= 1, before, 0.0)
            y_left = jnp.where(lane > 0, pltpu.roll(y, 1, 2), 0.0)
            down[start : start + SUB, 0] = jnp.where(
                (position >= 0) & (position < extent - 1), x, 0.0
            )
            center[start : start + SUB, 0] = jnp.where(
                inside, 1.0 - (x + before) - (y + y_left), 0.0
            )
            right[start : start + SUB, 0] = jnp.where(inside & (lane < LANES - 1), y, 0.0)
            left[start : start + SUB, 0] = jnp.where(inside, y_left, 0.0)
    loc_set = [coef_loc.at[n] for n in range(4)]
    static_set = [coef_static.at[n] for n in range(4)]

    for g in range(alpha_vregs):
        halo_wait(groups_a[g], 4 + g)
        result = diffuse(groups_a[g], (ping_a0, ping_a1), loc_set, height, 4)
        group_out(result, local_flat, g)

    def ensemble(owner):
        offset = pl.multiple_of(owner * span, span)
        total = None
        for m in range(members):
            base = pl.multiple_of(m * levels * height + owner * span, span)
            field = local_flat[pl.ds(base, span), :]
            term = field[None] * perturb[m, :, pl.ds(offset, span), :].astype(jnp.float32)
            total = term if total is None else total + term
        return total

    def pair_copy(k):
        return pltpu.make_async_remote_copy(
            src_ref=part_pair.at[k],
            dst_ref=pair_in.at[k],
            send_sem=pair_send.at[k],
            recv_sem=pair_recv.at[k],
            device_id={"mem": partner},
        )

    def chip_copy(k):
        return pltpu.make_async_remote_copy(
            src_ref=part_own.at[k],
            dst_ref=chip_in.at[k],
            send_sem=chip_send.at[k],
            recv_sem=chip_recv.at[k],
            device_id={"mem": lax.rem(chip + k, chips) * 2 + core},
        )

    order = list(range(1, chips)) + [0]
    for k in order:
        owner_chip = lax.rem(chip + k, chips)
        part_pair[k] = ensemble(owner_chip * 2 + (1 - core))
        pair_copy(k).start()
    for k in order:
        owner_chip = lax.rem(chip + k, chips)
        mine = ensemble(owner_chip * 2 + core)
        pair_copy(k).wait_recv()
        part_own[k] = mine + pair_in[k]
        if k > 0:
            chip_copy(k).start()

    lax.fori_loop(height // 2, height, cells, 0)
    halo_wait(field_s, 2)
    static_part = diffuse(field_s, (ping_s0, ping_s1), static_set, height, 4)
    for k in order:
        pair_copy(k).wait_send()
    total = part_own[0]
    for k in range(1, chips):
        chip_copy(k).wait_recv()
        total = total + chip_in[k]
    static_flat[0 : fields * height, :] = total.reshape(fields * height, LANES)
    for r in range(height):
        for b in range(static_vregs):
            at = pl.ds(b * SUB * height + r, SUB, stride=height)
            increment = static_flat[at, :] + static_part[halo + r, b]
            field_g[halo + r, b] = obs_scale[r, b] * increment - obs_shift[r, b]
    halo_start(field_g, 3)
    from_rows(field_g, static_flat, static_vregs)
    grads[0, 0] = static_flat[0 : fields * height, :].reshape(variables, span, LANES)

    def gather_copy(k):
        return pltpu.make_async_remote_copy(
            src_ref=grads.at[0, 0],
            dst_ref=grads.at[0, k],
            send_sem=gather_send.at[k],
            recv_sem=gather_recv.at[k],
            device_id={"mem": lax.rem(chip + k, chips) * 2 + core},
        )

    def relay_copy(k):
        return pltpu.make_async_remote_copy(
            src_ref=grads.at[0, k],
            dst_ref=grads.at[1, k],
            send_sem=relay_send.at[k],
            recv_sem=relay_recv.at[k],
            device_id={"mem": partner},
        )

    for k in range(1, chips):
        gather_copy(k).start()
    relay_copy(0).start()

    def project(way, k):
        source = lax.rem(chip + chips - k, chips) * 2 + (core if way == 0 else 1 - core)
        offset = pl.multiple_of(source * span, span)
        for m in range(members):
            base = pl.multiple_of(m * levels * height + source * span, span)
            total = None
            for v in range(variables):
                weight = perturb[m, v, pl.ds(offset, span), :].astype(jnp.float32)
                term = weight * grads[way, k, v]
                total = term if total is None else total + term
            local_flat[pl.ds(base, span), :] = total

    project(0, 0)
    halo_wait(field_g, 3)
    result = diffuse(field_g, (ping_s0, ping_s1), static_set, height, 4)
    from_rows(result, static_flat, static_vregs)
    out_static[...] = static_flat[0 : fields * height, :]

    for k in range(1, chips):
        gather_copy(k).wait_recv()
        relay_copy(k).start()
        project(0, k)
    for k in range(chips):
        relay_copy(k).wait_recv()
        project(1, k)
    for g in range(alpha_vregs):
        group_in(local_flat, g)
        halo_start(groups_b[g], 4 + alpha_vregs + g)
    for k in range(1, chips):
        chip_copy(k).wait_send()
        gather_copy(k).wait_send()
    for k in range(chips):
        relay_copy(k).wait_send()
    for g in range(alpha_vregs):
        halo_wait(groups_b[g], 4 + alpha_vregs + g)
        result = diffuse(groups_b[g], (ping_a0, ping_a1), loc_set, height, 4)
        group_out(result, out_alpha, g)


def update(field_a, mom_a, smooth_a, field_s, mom_s, smooth_s, new_a, new_mom_a, new_s, new_mom_s):
    for field, mom, smooth, new, new_mom in (
        (field_a, mom_a, smooth_a, new_a, new_mom_a),
        (field_s, mom_s, smooth_s, new_s, new_mom_s),
    ):
        moved = momentum_rate * mom[...] + (field[...] + smooth[...])
        new_mom[...] = moved
        new[...] = field[...] - step_rate * moved


def local(
    perturb,
    alpha,
    alpha_mom,
    static_ctl,
    static_mom,
    loc_coef,
    static_coef,
    obs_cell,
    obs_mask,
    obs_value,
    obs_weight,
):
    mem_count = lax.axis_size("mem")
    tile_count = lax.axis_size("tile")
    members, variables, levels, height, width = perturb.shape
    stations = obs_cell.shape[1]
    chips = mem_count // 2
    share = levels // mem_count
    fields = variables * share
    span = share * height
    alpha_vregs = members * levels // SUB
    static_vregs = -(-fields // SUB)
    rows = 2 * DIFF_STEPS + height + 4
    dims = (mem_count, tile_count, members, variables, levels, height, stations)
    f32 = jnp.float32
    vmem = pl.BlockSpec(memory_space=pltpu.VMEM)
    in_hbm = pl.BlockSpec(memory_space=pltpu.HBM)
    dma = pltpu.SemaphoreType.DMA
    chunk = (chips, variables, span, width)
    alpha_smooth, static_smooth, own_ctl = pl.pallas_call(
        functools.partial(kernel, dims),
        out_shape=(
            jax.ShapeDtypeStruct((members * levels * height, width), f32),
            jax.ShapeDtypeStruct((fields * height, width), f32),
            jax.ShapeDtypeStruct((variables, share, height, width), f32),
        ),
        in_specs=[in_hbm] * 9,
        out_specs=(vmem,) * 3,
        scratch_shapes=[
            pltpu.VMEM((members * levels * height, width), f32),
            pltpu.VMEM((members, variables, levels * height, width), perturb.dtype),
            pltpu.VMEM(obs_cell.shape, obs_cell.dtype),
            pltpu.VMEM(obs_mask.shape, obs_mask.dtype),
            pltpu.VMEM((alpha_vregs, rows, 1, SUB, width), f32),
            pltpu.VMEM((alpha_vregs, rows, 1, SUB, width), f32),
            pltpu.VMEM((rows, 1, SUB, width), f32),
            pltpu.VMEM((rows, 1, SUB, width), f32),
            pltpu.VMEM((rows, static_vregs, SUB, width), f32),
            pltpu.VMEM((rows, static_vregs, SUB, width), f32),
            pltpu.VMEM((rows, static_vregs, SUB, width), f32),
            pltpu.VMEM((rows, static_vregs, SUB, width), f32),
            pltpu.VMEM((SUB * height, width), f32),
            pltpu.VMEM((rows, SUB, width), f32),
            pltpu.VMEM((4, rows, 1, SUB, width), f32),
            pltpu.VMEM((4, rows, 1, SUB, width), f32),
            pltpu.VMEM((variables, share, 1, stations), f32),
            pltpu.VMEM((variables, share, 1, stations), f32),
            pltpu.VMEM((2 * static_vregs * SUB, stations), f32),
            pltpu.VMEM((height, static_vregs, SUB, width), f32),
            pltpu.VMEM((height, static_vregs, SUB, width), f32),
            pltpu.VMEM((static_vregs * SUB * height, width), f32),
            pltpu.VMEM((members * levels * height, width), f32),
            pltpu.VMEM(chunk, f32),
            pltpu.VMEM(chunk, f32),
            pltpu.VMEM(chunk, f32),
            pltpu.VMEM(chunk, f32),
            pltpu.VMEM((2,) + chunk, f32),
            dma((9,)),
            dma((4 + 2 * alpha_vregs, 2)),
            dma((4 + 2 * alpha_vregs, 2)),
            dma((chips,)),
            dma((chips,)),
            dma((chips,)),
            dma((chips,)),
            dma((chips,)),
            dma((chips,)),
            dma((chips,)),
            dma((chips,)),
        ],
        compiler_params=pltpu.CompilerParams(
            collective_id=0, has_side_effects=True, vmem_limit_bytes=60 * 1024 * 1024
        ),
        name="analysis",
    )(
        perturb.reshape(members, variables, levels * height, width),
        alpha.reshape(members * levels * height, width),
        loc_coef.reshape(2 * height, width),
        static_coef.reshape(2 * height, width),
        obs_cell,
        obs_mask,
        static_ctl,
        obs_value,
        obs_weight,
    )
    like = jax.ShapeDtypeStruct
    new_alpha, new_alpha_mom, new_static, new_static_mom = pl.pallas_call(
        update,
        out_shape=(like(alpha.shape, f32),) * 2 + (like(own_ctl.shape, f32),) * 2,
        in_specs=[vmem] * 6,
        out_specs=(vmem,) * 4,
        compiler_params=pltpu.CompilerParams(vmem_limit_bytes=60 * 1024 * 1024),
        name="update",
    )(
        alpha,
        alpha_mom,
        alpha_smooth.reshape(alpha.shape),
        own_ctl,
        static_mom,
        static_smooth.reshape(own_ctl.shape),
    )
    return (new_alpha, new_alpha_mom, new_static, new_static_mom)


def solution(mesh):
    return jax.shard_map(
        local,
        mesh=mesh,
        in_specs=(
            P("mem", None, None, "tile", None),
            P("mem", None, "tile", None),
            P("mem", None, "tile", None),
            P(None, None, "tile", None),
            P(None, "mem", "tile", None),
            P(None, "tile", None),
            P(None, "tile", None),
            P("tile", None),
            P("tile", None),
            P(None, None, "tile", None),
            P(None, None, "tile", None),
        ),
        out_specs=(
            P("mem", None, "tile", None),
            P("mem", None, "tile", None),
            P(None, "mem", "tile", None),
            P(None, "mem", "tile", None),
        ),
        check_vma=False,
    )
```
